32 devices in a mesh: head: 8 (over y, x, core), key: 4 (over z).
Axes of the slice: x: 2, y: 2, z: 4, core: 2. Of those that a mesh axis runs over, the one named last changes fastest.
Arguments:
- queries: bfloat16 [128, 128, 192], P(None, 'head'), may hold values from -16 to 16
- w_uk: bfloat16 [128, 128, 512], P('head'), may hold values from -0.5 to 0.5
- w_uv: bfloat16 [128, 512, 128], P('head'), may hold values from -0.25 to 0.25
- latent: bfloat16 [8192, 576], P('key'), may hold values from -5 to 5
- out_grad: bfloat16 [128, 128, 128], P(None, 'head'), may hold values from -6 to 6
- offsets: int32 [128], replicated, may hold values from 2048 to 8191, as said below
Outputs:
- d_queries: bfloat16 [128, 128, 192], P('key', 'head')
- d_latent: bfloat16 [8192, 576], P('key')
The draws below stay inside these ranges and needn't reach their ends.
Inputs may be any that keep to these rules, and one draw needn't show every extreme that they name: Row r sees keys 0 to offsets[r].
All inputs are finite; a program needn't handle non-finite values.
Results may differ from the reference program's by a relative error of at most 0.0079.
Values may be sent and summed in bfloat16 or wider, within the bound.
A program may use at most 128 MiB of HBM per device.

```python
import math
import jax
import jax.numpy as jnp
from jax import lax

H = 128
DN = 128
DR = 64
DC = 512
DV = 128
R = 128
S = 8192


def draw_queries(key, part):
    inner = jax.random.fold_in(key, 11)
    base = jnp.clip(jax.random.normal(inner, (R, H, DN + DR), jnp.float32), -4.0, 4.0)
    return base.astype(jnp.bfloat16)


def draw_latent(key, part):
    inner = jax.random.fold_in(key, 13)
    fraction = jnp.arange(S, dtype=jnp.float32) / S
    base = jnp.clip(jax.random.normal(inner, (S, DC + DR), jnp.float32), -4.0, 4.0) * (0.75 + 0.5 * fraction)[:, None]
    return base.astype(jnp.bfloat16)


def draw_offsets(key, part):
    inner = jax.random.fold_in(key, 17)
    first, second = jax.random.split(inner)
    values = jax.random.randint(first, (R,), S // 4, S)
    order = jax.random.permutation(second, R)
    return values.at[order[0]].set(S - 1).at[order[1]].set(S // 4)


def steps_of(key, shape, shards, smallest, high):
    loudness = 1.0
    for position, shards_of in shards:
        steps = jax.random.uniform(jax.random.fold_in(jax.random.fold_in(key, 6), position), (shards_of,), jnp.float32, smallest / len(shards), high / len(shards))
        loudness = loudness * jnp.repeat(jnp.exp(steps), shape[position] // shards_of).reshape((-1,) + (1,) * (len(shape) - 1 - position))
    return loudness


def centred(key, dims, deviation, most, pieces=(), kind=jnp.bfloat16):
    loudness = steps_of(key, dims, pieces, -0.22, 0.18) if pieces else 1.0
    result = jax.random.normal(key, dims, jnp.float32) * deviation * loudness
    return jnp.minimum(jnp.maximum(result, -most), most).astype(kind)


def setup_inputs(seed: int = 0) -> dict:
    splits = jax.random.split(jax.random.key(seed), 7)
    queries = draw_queries(jax.random.fold_in(splits[6], 71), 0)
    w_uk = centred(splits[1], (H, DN, DC), DN ** -0.5, 0.5, ((0, 8),))
    w_uv = centred(splits[2], (H, DC, DV), DC ** -0.5, 0.25, ((0, 8),))
    latent = draw_latent(jax.random.fold_in(splits[6], 71), 0)
    out_grad = centred(splits[4], (R, H, DV), 1.0, 6.0, ((1, 8),))
    offsets = draw_offsets(jax.random.fold_in(splits[6], 71), 0)
    return dict(queries=queries, w_uk=w_uk, w_uv=w_uv, latent=latent, out_grad=out_grad, offsets=offsets)


floor_score = -1e+30

def reference(queries, w_uk, w_uv, latent, out_grad, offsets):
    scale = 1.0 / math.sqrt(DN + DR)
    visible = jnp.arange(S, dtype=jnp.int32)[None, :] <= offsets[:, None]
    values = latent[:, :DC]

    def per_head(carry, inputs):
        q_head, up_key, up_value, grad = inputs
        q_lat = jnp.dot(q_head[:, :DN], up_key, preferred_element_type=jnp.float32).astype(jnp.bfloat16)
        q_cat = jnp.concatenate([q_lat, q_head[:, DN:]], axis=1)
        d_lat = jnp.dot(grad, up_value.T, preferred_element_type=jnp.float32).astype(jnp.bfloat16)
        scores = jnp.dot(q_cat, latent.T, preferred_element_type=jnp.float32) * scale
        scores = jnp.where(visible, scores, floor_score)
        top = lax.optimization_barrier(jnp.max(scores, axis=1))
        total = lax.optimization_barrier(jnp.sum(jnp.where(visible, jnp.exp(scores - top[:, None]), 0.0), axis=1))
        log_norm = top + jnp.log(total)
        probs = jnp.where(visible, jnp.exp(scores - log_norm[:, None]), 0.0)
        d_probs = jnp.dot(d_lat, values.T, preferred_element_type=jnp.float32)
        delta = lax.optimization_barrier(jnp.sum(probs * d_probs, axis=1))
        d_scores = (probs * (d_probs - delta[:, None])).astype(jnp.bfloat16)
        dq_lat = jnp.dot(d_scores, latent, preferred_element_type=jnp.float32) * scale
        dq_nope = jnp.dot(dq_lat[:, :DC], up_key.astype(jnp.float32).T, precision=lax.Precision.HIGHEST)
        dq_head = jnp.concatenate([dq_nope, dq_lat[:, DC:]], axis=1).astype(jnp.bfloat16)
        from_scores = jnp.dot(d_scores.T, q_cat, preferred_element_type=jnp.float32) * scale
        from_values = jnp.dot(probs.astype(jnp.bfloat16).T, d_lat, preferred_element_type=jnp.float32)
        carry = carry + jnp.concatenate([from_scores[:, :DC] + from_values, from_scores[:, DC:]], axis=1)
        return (carry, dq_head)
    start = jnp.zeros((S, DC + DR), jnp.float32)
    summed, dq_all = lax.scan(per_head, start, (jnp.transpose(queries, (1, 0, 2)), w_uk, w_uv, jnp.transpose(out_grad, (1, 0, 2))))
    return (jnp.transpose(dq_all, (1, 0, 2)), summed.astype(jnp.bfloat16))
```

```python
import functools
import math

import jax
import jax.numpy as jnp
from jax import lax
from jax.experimental import pallas as pl
from jax.experimental.pallas import tpu as pltpu
from jax.sharding import PartitionSpec as P

floor_score = -1e30
MESH = pl.DeviceIdType.MESH
f32 = jnp.float32
bf16 = jnp.bfloat16
VMEM_BYTES = 60 * 1024 * 1024


def dot(a, b):
    return lax.dot_general(a, b, (((1,), (0,)), ((), ())), preferred_element_type=f32)


def dot_t(a, b):
    return lax.dot_general(a, b, (((1,), (1,)), ((), ())), preferred_element_type=f32)


def scores_kernel(
    scale, group, tile, q_ref, og_ref, uk_ref, uv_ref, lat_ref, off_ref,
    e_ref, dp_ref, qc_ref, dl_ref, st_ref, s_ref,
):
    step = pl.program_id(0)
    rows = q_ref.shape[1]
    nope = uk_ref.shape[1]
    width = uk_ref.shape[2]
    keys = lat_ref.shape[0]
    for h in range(group):
        at = pl.ds(h * rows, rows)
        qc_ref[at, :width] = dot(q_ref[h, :, :nope], uk_ref[h]).astype(bf16)
        qc_ref[at, width:] = q_ref[h, :, nope:]
        dl_ref[at, :] = dot_t(og_ref[h], uv_ref[h]).astype(bf16)
    qc = qc_ref[...]
    dl = dl_ref[...]
    off = jnp.concatenate([off_ref[...]] * group, axis=1)
    top = jnp.full((1, group * rows), floor_score, f32)
    for t in range(keys // tile):
        at = pl.ds(t * tile, tile)
        s = dot_t(lat_ref[at, :], qc) * scale
        position = lax.broadcasted_iota(jnp.int32, s.shape, 0) + t * tile
        s = jnp.where(position <= off, s, floor_score)
        s_ref[at, :] = s
        top = jnp.maximum(top, jnp.max(s, axis=0, keepdims=True))
        dp_ref[at, :] = dot_t(lat_ref[at, :width], dl).astype(bf16)
    shift = jnp.maximum(top, 0.5 * floor_score)
    total = jnp.zeros((1, group * rows), f32)
    acc = jnp.zeros((1, group * rows), f32)
    for t in range(keys // tile):
        at = pl.ds(t * tile, tile)
        e = jnp.exp(s_ref[at, :] - shift).astype(bf16)
        e_ref[at, :] = e
        e = e.astype(f32)
        total = total + jnp.sum(e, axis=0, keepdims=True)
        acc = acc + jnp.sum(e * dp_ref[at, :].astype(f32), axis=0, keepdims=True)
    for h in range(group):
        cut = slice(h * rows, (h + 1) * rows)
        at = pl.ds(step * group + h, 1)
        st_ref[0, at, :] = shift[:, cut]
        st_ref[1, at, :] = total[:, cut]
        st_ref[2, at, :] = acc[:, cut]


def stats_kernel(key_n, st_ref, out_ref, got_ref, send_sem, recv_sem):
    me = lax.axis_index("key")
    barrier = pltpu.get_barrier_semaphore()
    for d in range(1, key_n):
        pl.semaphore_signal(
            barrier, inc=1, device_id={"key": lax.rem(me + d, key_n)}, device_id_type=MESH
        )
    pl.semaphore_wait(barrier, key_n - 1)
    copies = []
    for d in range(1, key_n):
        copy = pltpu.make_async_remote_copy(
            src_ref=st_ref,
            dst_ref=got_ref.at[d - 1],
            send_sem=send_sem.at[d - 1],
            recv_sem=recv_sem.at[d - 1],
            device_id={"key": lax.rem(me + d, key_n)},
            device_id_type=MESH,
        )
        copy.start()
        copies.append(copy)
    for copy in copies:
        copy.wait()
    mine = st_ref[0]
    top = mine
    for d in range(key_n - 1):
        top = jnp.maximum(top, got_ref[d, 0])
    near = jnp.exp(mine - top)
    total = near * st_ref[1]
    acc = near * st_ref[2]
    for d in range(key_n - 1):
        part = jnp.exp(got_ref[d, 0] - top)
        total = total + part * got_ref[d, 1]
        acc = acc + part * got_ref[d, 2]
    out_ref[0] = near / total
    out_ref[1] = acc / total


def grads_kernel(
    scale, key_n, rows, tile, e_ref, dp_ref, norm_ref, delta_ref, qc_ref, dl_ref, lt_ref, uk_ref,
    dlat_ref, dq_ref, ds_ref, p_ref, acc_ref,
):
    step = pl.program_id(0)
    width = dl_ref.shape[1]
    nope = uk_ref.shape[1]
    wide = e_ref.shape[1]
    for t in range(wide // tile):
        cut = slice(t * tile, (t + 1) * tile)
        p = e_ref[:, cut].astype(f32) * norm_ref[:, cut]
        p_ref[:, cut] = p.astype(bf16)
        ds_ref[:, cut] = (p * (dp_ref[:, cut].astype(f32) - delta_ref[:, cut])).astype(bf16)
        part = dot(lt_ref[...], ds_ref[:, cut])

        @pl.when(step == 0)
        def _():
            acc_ref[:, cut] = part

        @pl.when(step > 0)
        def _():
            acc_ref[:, cut] += part

    from_scores = dot(ds_ref[...], qc_ref[...]) * scale
    from_values = dot(p_ref[...], dl_ref[...])
    dlat_ref[:, :width] = (from_scores[:, :width] + from_values).astype(bf16)
    dlat_ref[:, width:] = from_scores[:, width:].astype(bf16)

    @pl.when(step == pl.num_programs(0) - 1)
    def _():
        chunk = rows // key_n
        for h in range(wide // rows):
            cut = slice(h * rows, (h + 1) * rows)
            x = acc_ref[:width, cut] * scale
            high = x.astype(bf16)
            low = (x - high.astype(f32)).astype(bf16)
            w = uk_ref[h]
            a = (dot(w, high) + dot(w, low)).T
            b = (acc_ref[width:, cut] * scale).T
            for j in range(key_n):
                at = slice(j * chunk, (j + 1) * chunk)
                dq_ref[j, h, :, :nope] = a[at].astype(bf16)
                dq_ref[j, h, :, nope:] = b[at].astype(bf16)


def joins_kernel(
    key_n, head_n, dlat_ref, dq_ref, out_ref, dqo_ref, work_ref, got_ref, dqg_ref,
    rs_send, rs_recv, ag_send, ag_recv, q_send, q_recv,
):
    mk = lax.axis_index("key")
    mh = lax.axis_index("head")
    bits = head_n.bit_length() - 1
    keys = dlat_ref.shape[0]

    def bit(b):
        return lax.rem(lax.div(mh, 1 << b), 2)

    def partner(b):
        return mh + (1 - 2 * bit(b)) * (1 << b)

    barrier = pltpu.get_barrier_semaphore()
    for d in range(1, key_n):
        pl.semaphore_signal(
            barrier, inc=1, device_id={"key": lax.rem(mk + d, key_n)}, device_id_type=MESH
        )
    for b in range(bits):
        pl.semaphore_signal(
            barrier, inc=1, device_id={"head": partner(b)}, device_id_type=MESH
        )
    pl.semaphore_wait(barrier, key_n - 1 + bits)

    def remote(src, dst, send, recv, where):
        copy = pltpu.make_async_remote_copy(
            src_ref=src, dst_ref=dst, send_sem=send, recv_sem=recv,
            device_id=where, device_id_type=MESH,
        )
        copy.start()
        return copy

    q_copies = []
    for d in range(1, key_n):
        to = lax.rem(mk + d, key_n)
        q_copies.append(
            remote(dq_ref.at[to], dqg_ref.at[d - 1], q_send.at[d - 1], q_recv.at[d - 1], {"key": to})
        )
    orders = [[0] + list(range(1, bits)), [0] + list(range(bits - 1, 0, -1))]
    base = [0, keys // 2]
    place = [0, keys // 2]
    length = keys // 2
    for i in range(bits):
        half = length // 2
        copies = []
        source = dlat_ref if i == 0 else work_ref
        for s in range(2):
            b = orders[s][i]
            v = bit(b)
            away = pl.multiple_of(base[s] + (1 - v) * half, half)
            copies.append(
                remote(
                    source.at[pl.ds(away, half)], got_ref.at[pl.ds(place[s], half)],
                    rs_send.at[s, i], rs_recv.at[s, i], {"head": partner(b)},
                )
            )
            base[s] = pl.multiple_of(base[s] + v * half, half)
        for s in range(2):
            copies[s].wait()
            kept = pl.ds(base[s], half)
            summed = source[kept, :].astype(f32) + got_ref[pl.ds(place[s], half), :].astype(f32)
            if i == bits - 1:
                out_ref[kept, :] = summed.astype(bf16)
            else:
                work_ref[kept, :] = summed.astype(bf16)
            place[s] = place[s] + half
        length = half
    for i in range(bits - 1, -1, -1):
        copies = []
        for s in range(2):
            b = orders[s][i]
            at = pl.ds(base[s], length)
            copies.append(
                remote(
                    out_ref.at[at], out_ref.at[at],
                    ag_send.at[s, i], ag_recv.at[s, i], {"head": partner(b)},
                )
            )
        for s in range(2):
            copies[s].wait()
            base[s] = pl.multiple_of(base[s] - bit(orders[s][i]) * length, length)
        length = 2 * length
    for copy in q_copies:
        copy.wait()
    summed = dq_ref[mk].astype(f32)
    for d in range(key_n - 1):
        summed = summed + dqg_ref[d].astype(f32)
    dqo_ref[...] = summed.astype(bf16)


def vmem(shape=None, index=None):
    return pl.BlockSpec(shape, index, memory_space=pltpu.VMEM)


def shards(key_n, head_n, queries, w_uk, w_uv, latent, out_grad, offsets):
    rows, heads, width = queries.shape
    keys, full = latent.shape
    nope = w_uk.shape[1]
    lat = w_uk.shape[2]
    values = out_grad.shape[2]
    scale = 1.0 / math.sqrt(width)
    wide = heads * rows
    group = 4 if heads % 4 == 0 else heads
    span = group * rows
    tile = min(512, keys)
    whole2 = lambda i: (0, 0)
    off = (offsets - lax.axis_index("key") * keys).reshape(1, rows)
    e, dp, qc, dl, st = pl.pallas_call(
        functools.partial(scores_kernel, scale, group, tile),
        grid=(heads // group,),
        in_specs=[
            vmem((group, rows, width), lambda i: (i, 0, 0)),
            vmem((group, rows, values), lambda i: (i, 0, 0)),
            vmem((group, nope, lat), lambda i: (i, 0, 0)),
            vmem((group, lat, values), lambda i: (i, 0, 0)),
            vmem((keys, full), whole2),
            vmem((1, rows), whole2),
        ],
        out_specs=[
            vmem((keys, span), lambda i: (0, i)),
            vmem((keys, span), lambda i: (0, i)),
            vmem((span, full), lambda i: (i, 0)),
            vmem((span, lat), lambda i: (i, 0)),
            vmem((3, heads, rows), lambda i: (0, 0, 0)),
        ],
        out_shape=[
            jax.ShapeDtypeStruct((keys, wide), bf16),
            jax.ShapeDtypeStruct((keys, wide), bf16),
            jax.ShapeDtypeStruct((wide, full), bf16),
            jax.ShapeDtypeStruct((wide, lat), bf16),
            jax.ShapeDtypeStruct((3, heads, rows), f32),
        ],
        scratch_shapes=[pltpu.VMEM((keys, span), f32)],
        compiler_params=pltpu.CompilerParams(vmem_limit_bytes=VMEM_BYTES),
    )(queries.transpose(1, 0, 2), out_grad.transpose(1, 0, 2), w_uk, w_uv, latent, off)
    joined = pl.pallas_call(
        functools.partial(stats_kernel, key_n),
        in_specs=[vmem()],
        out_specs=vmem(),
        out_shape=jax.ShapeDtypeStruct((2, heads, rows), f32),
        scratch_shapes=[
            pltpu.VMEM((key_n - 1, 3, heads, rows), f32),
            pltpu.SemaphoreType.DMA((key_n - 1,)),
            pltpu.SemaphoreType.DMA((key_n - 1,)),
        ],
        compiler_params=pltpu.CompilerParams(collective_id=0, has_side_effects=True),
    )(st)
    joined = joined.reshape(2, 1, wide)
    chunk = rows // key_n
    dlat, dq = pl.pallas_call(
        functools.partial(grads_kernel, scale, key_n, rows, min(512, wide)),
        grid=(keys // tile,),
        in_specs=[
            vmem((tile, wide), lambda i: (i, 0)),
            vmem((tile, wide), lambda i: (i, 0)),
            vmem((1, wide), whole2),
            vmem((1, wide), whole2),
            vmem((wide, full), whole2),
            vmem((wide, lat), whole2),
            vmem((full, tile), lambda i: (0, i)),
            vmem((heads, nope, lat), lambda i: (0, 0, 0)),
        ],
        out_specs=[
            vmem((tile, full), lambda i: (i, 0)),
            vmem((key_n, heads, chunk, width), lambda i: (0, 0, 0, 0)),
        ],
        out_shape=[
            jax.ShapeDtypeStruct((keys, full), bf16),
            jax.ShapeDtypeStruct((key_n, heads, chunk, width), bf16),
        ],
        scratch_shapes=[
            pltpu.VMEM((tile, wide), bf16),
            pltpu.VMEM((tile, wide), bf16),
            pltpu.VMEM((full, wide), f32),
        ],
        compiler_params=pltpu.CompilerParams(vmem_limit_bytes=VMEM_BYTES),
    )(e, dp, joined[0], joined[1], qc, dl, latent.T, w_uk)
    bits = head_n.bit_length() - 1
    d_latent, dq_sum = pl.pallas_call(
        functools.partial(joins_kernel, key_n, head_n),
        in_specs=[vmem(), vmem()],
        out_specs=[vmem(), vmem()],
        out_shape=[
            jax.ShapeDtypeStruct((keys, full), bf16),
            jax.ShapeDtypeStruct((heads, chunk, width), bf16),
        ],
        scratch_shapes=[
            pltpu.VMEM((keys, full), bf16),
            pltpu.VMEM((keys, full), bf16),
            pltpu.VMEM((key_n - 1, heads, chunk, width), bf16),
            pltpu.SemaphoreType.DMA((2, bits)),
            pltpu.SemaphoreType.DMA((2, bits)),
            pltpu.SemaphoreType.DMA((2, bits)),
            pltpu.SemaphoreType.DMA((2, bits)),
            pltpu.SemaphoreType.DMA((key_n - 1,)),
            pltpu.SemaphoreType.DMA((key_n - 1,)),
        ],
        compiler_params=pltpu.CompilerParams(
            vmem_limit_bytes=VMEM_BYTES, collective_id=1, has_side_effects=True
        ),
    )(dlat, dq)
    return (dq_sum.transpose(1, 0, 2), d_latent)


def solution(mesh):
    return jax.shard_map(
        functools.partial(shards, mesh.shape["key"], mesh.shape["head"]),
        mesh=mesh,
        in_specs=(
            P(None, "head", None),
            P("head", None, None),
            P("head", None, None),
            P("key", None),
            P(None, "head", None),
            P(),
        ),
        out_specs=(P("key", "head", None), P("key", None)),
        check_vma=False,
    )
```

```python
import functools
import math

import jax
import jax.numpy as jnp
from jax import lax
from jax.experimental import pallas as pl
from jax.experimental.pallas import tpu as pltpu
from jax.sharding import PartitionSpec as P

floor_score = -1e30
MESH = pl.DeviceIdType.MESH
f32 = jnp.float32
bf16 = jnp.bfloat16
VMEM_BYTES = 60 * 1024 * 1024
TILE = 512
BLOCK = 512


def dot(a, b):
    return lax.dot_general(a, b, (((1,), (0,)), ((), ())), preferred_element_type=f32)


def dot_t(a, b):
    return lax.dot_general(a, b, (((1,), (1,)), ((), ())), preferred_element_type=f32)


def dot_c(a, b):
    return lax.dot_general(a, b, (((0,), (0,)), ((), ())), preferred_element_type=f32)


def scores_kernel(
    scale, group, tile, q_ref, og_ref, uk_ref, uv_ref, lt_ref, off_ref,
    e_ref, dp_ref, qc_ref, dl_ref, st_ref, tops_ref, lat_ref,
):
    step = pl.program_id(0)
    rows = q_ref.shape[2]
    nope = uk_ref.shape[1]
    width = uk_ref.shape[2]
    keys = lt_ref.shape[1]

    @pl.when(step == 0)
    def _():
        lat_ref[...] = lt_ref[...].T

    for h in range(group):
        cut = slice(h * rows, (h + 1) * rows)
        qc_ref[:width, cut] = dot_c(uk_ref[h], q_ref[h, :nope, :]).astype(bf16)
        qc_ref[width:, cut] = q_ref[h, nope:, :]
        dl_ref[:, cut] = dot_t(uv_ref[h], og_ref[h]).astype(bf16)
    qc = qc_ref[...]
    dl = dl_ref[...]
    off = jnp.concatenate([off_ref[...]] * group, axis=1)
    tops = []
    totals = []
    accs = []
    for t in range(keys // tile):
        at = pl.ds(t * tile, tile)
        s = dot(lat_ref[at, :], qc) * scale
        dp = dot(lat_ref[at, :width], dl).astype(bf16)
        position = lax.broadcasted_iota(jnp.int32, s.shape, 0)
        s = jnp.where(position <= off - t * tile, s, floor_score)
        top = jnp.maximum(jnp.max(s, axis=0, keepdims=True), 0.5 * floor_score)
        e = jnp.exp(s - top).astype(bf16)
        e_ref[at, :] = e
        dp_ref[at, :] = dp
        e = e.astype(f32)
        tops.append(top)
        totals.append(jnp.sum(e, axis=0, keepdims=True))
        accs.append(jnp.sum(e * dp.astype(f32), axis=0, keepdims=True))
    best = functools.reduce(jnp.maximum, tops)
    total = 0.0
    acc = 0.0
    for top, a, b in zip(tops, totals, accs):
        near = jnp.exp(top - best)
        total = total + near * a
        acc = acc + near * b
    for h in range(group):
        cut = slice(h * rows, (h + 1) * rows)
        at = pl.ds(step * group + h, 1)
        st_ref[0, at, :] = best[:, cut]
        st_ref[1, at, :] = total[:, cut]
        st_ref[2, at, :] = acc[:, cut]
        for t, top in enumerate(tops):
            tops_ref[t, at, :] = top[:, cut]


def grads_kernel(
    scale, key_n, head_n, rows, tile, block, group,
    e_hbm, dp_hbm, qc_hbm, dl_hbm, lt_hbm, uk_hbm, st_ref, tops_ref,
    out_ref, dqo_ref,
    e_ref, dp_ref, qc_ref, dl_ref, lt_ref, uk_ref, norm_ref, delta_ref, part_ref, got_ref,
    dq_ref, dqg_ref, stg_ref,
    e_sem, dp_sem, in_sem, st_send, st_recv, rs_send, rs_recv, ag_send, ag_recv, q_send, q_recv,
):
    mk = lax.axis_index("key")
    mh = lax.axis_index("head")
    bits = head_n.bit_length() - 1
    keys = e_ref.shape[0]
    wide = e_ref.shape[1]
    width = dl_ref.shape[0]
    nope = uk_ref.shape[1]
    full = qc_ref.shape[0]
    blocks = keys // block
    span = group * rows
    groups = wide // span
    piece = full // head_n
    chunk = rows // key_n

    def bit(b):
        return lax.rem(lax.div(mh, 1 << b), 2)

    def partner(b):
        return mh + (1 - 2 * bit(b)) * (1 << b)

    barrier = pltpu.get_barrier_semaphore()
    for d in range(1, key_n):
        pl.semaphore_signal(
            barrier, inc=1, device_id={"key": lax.rem(mk + d, key_n)}, device_id_type=MESH
        )
    for b in range(bits):
        pl.semaphore_signal(
            barrier, inc=1, device_id={"head": partner(b)}, device_id_type=MESH
        )

    def local(a, b, sem):
        copy = pltpu.make_async_copy(a, b, sem)
        copy.start()
        return copy

    e_in = []
    dp_in = []
    weights = []
    for b in range(blocks):
        at = pl.ds(b * block, block)
        e_in.append(local(e_hbm.at[at], e_ref.at[at], e_sem.at[b]))
        dp_in.append(local(dp_hbm.at[at], dp_ref.at[at], dp_sem.at[b]))
        if b == 0:
            weights.append(local(qc_hbm, qc_ref, in_sem.at[0]))
            weights.append(local(dl_hbm, dl_ref, in_sem.at[1]))
    weights.append(local(lt_hbm, lt_ref, in_sem.at[2]))
    weights.append(local(uk_hbm, uk_ref, in_sem.at[3]))

    pl.semaphore_wait(barrier, key_n - 1 + bits)

    def remote(src, dst, send, recv, where):
        copy = pltpu.make_async_remote_copy(
            src_ref=src, dst_ref=dst, send_sem=send, recv_sem=recv,
            device_id=where, device_id_type=MESH,
        )
        copy.start()
        return copy

    copies = []
    for d in range(1, key_n):
        copies.append(
            remote(
                st_ref, stg_ref.at[d - 1], st_send.at[d - 1], st_recv.at[d - 1],
                {"key": lax.rem(mk + d, key_n)},
            )
        )
    for copy in copies:
        copy.wait()
    best = st_ref[0]
    for d in range(key_n - 1):
        best = jnp.maximum(best, stg_ref[d, 0])
    near = jnp.exp(st_ref[0] - best)
    total = near * st_ref[1]
    acc = near * st_ref[2]
    for d in range(key_n - 1):
        near = jnp.exp(stg_ref[d, 0] - best)
        total = total + near * stg_ref[d, 1]
        acc = acc + near * stg_ref[d, 2]
    delta_ref[...] = acc / total
    for t in range(keys // tile):
        norm_ref[t] = jnp.exp(tops_ref[t] - best) / total

    def row(ref, g, t=None):
        pick = (lambda i: ref[pl.ds(i, 1), :]) if t is None else (lambda i: ref[t, pl.ds(i, 1), :])
        return jnp.concatenate([pick(g * group + h) for h in range(group)], axis=1)

    def latent_block(b):
        e_in[b].wait()
        dp_in[b].wait()
        if b == 0:
            weights[0].wait()
            weights[1].wait()
        at = pl.ds(b * block, block)
        for g in range(groups):
            cut = slice(g * span, (g + 1) * span)
            p = e_ref[at, cut].astype(f32) * row(norm_ref, g, b * block // tile)
            e_ref[at, cut] = p.astype(bf16)
            dp_ref[at, cut] = (p * (dp_ref[at, cut].astype(f32) - row(delta_ref, g))).astype(bf16)
        from_scores = dot_t(qc_ref[...], dp_ref[at, :]) * scale
        from_values = dot_t(dl_ref[...], e_ref[at, :])
        summed = jnp.concatenate(
            [from_scores[:width] + from_values, from_scores[width:]], axis=0
        )
        for j in range(head_n):
            part_ref[b, j] = summed[j * piece : (j + 1) * piece].astype(bf16)

    q_copies = []

    def query_group(g):
        if g == 0:
            weights[2].wait()
            weights[3].wait()
        cut = slice(g * span, (g + 1) * span)
        dq = dot(lt_ref[...], dp_ref[:, cut]) * scale
        high = dq[:width].astype(bf16)
        low = (dq[:width] - high.astype(f32)).astype(bf16)
        for h in range(group):
            mine = slice(h * rows, (h + 1) * rows)
            w = uk_ref[g * group + h]
            a = (dot(w, high[:, mine]) + dot(w, low[:, mine])).T
            r = dq[width:, mine].T
            for j in range(key_n):
                at = slice(j * chunk, (j + 1) * chunk)
                dq_ref[j, g, h, :, :nope] = a[at].astype(bf16)
                dq_ref[j, g, h, :, nope:] = r[at].astype(bf16)
        for d in range(1, key_n):
            to = lax.rem(mk + d, key_n)
            q_copies.append(
                remote(
                    dq_ref.at[to, g], dqg_ref.at[d - 1, g],
                    q_send.at[d - 1, g], q_recv.at[d - 1, g], {"key": to},
                )
            )

    orders = [[0] + list(range(1, bits)), [0] + list(range(bits - 1, 0, -1))]
    flight = [None] * blocks
    base = [0] * blocks
    stage = [0] * blocks

    def advance(b):
        k = stage[b]
        order = orders[b % 2]
        if k > 0:
            flight[b].wait()
        if 0 < k <= bits:
            size = head_n >> k
            spot = head_n - (head_n >> (k - 1))
            for j in range(size):
                summed = part_ref[b, base[b] + j].astype(f32) + got_ref[b, spot + j].astype(f32)
                if k == bits:
                    out_ref[b, base[b] + j] = summed.astype(bf16)
                else:
                    part_ref[b, base[b] + j] = summed.astype(bf16)
        if k < bits:
            size = head_n >> (k + 1)
            spot = head_n - (head_n >> k)
            v = bit(order[k])
            flight[b] = remote(
                part_ref.at[b, pl.ds(base[b] + (1 - v) * size, size)],
                got_ref.at[b, pl.ds(spot, size)],
                rs_send.at[b, k], rs_recv.at[b, k], {"head": partner(order[k])},
            )
            base[b] = base[b] + v * size
        elif k < 2 * bits:
            i = k - bits
            size = 1 << i
            if i > 0:
                base[b] = base[b] - bit(order[bits - i]) * (size // 2)
            at = pl.ds(base[b], size)
            flight[b] = remote(
                out_ref.at[b, at], out_ref.at[b, at],
                ag_send.at[b, i], ag_recv.at[b, i], {"head": partner(order[bits - 1 - i])},
            )
        stage[b] = k + 1

    def sweep(last):
        for b in range(last):
            if stage[b] <= 2 * bits:
                advance(b)

    for b in range(blocks):
        latent_block(b)
        sweep(b + 1)
    for g in range(groups):
        query_group(g)
        sweep(blocks)
    while min(stage) <= 2 * bits:
        sweep(blocks)
    for copy in q_copies:
        copy.wait()
    for g in range(groups):
        summed = dq_ref[mk, g].astype(f32)
        for d in range(key_n - 1):
            summed = summed + dqg_ref[d, g].astype(f32)
        dqo_ref[g] = summed.astype(bf16)


def vmem(shape=None, index=None):
    return pl.BlockSpec(shape, index, memory_space=pltpu.VMEM)


def shards(key_n, head_n, queries, w_uk, w_uv, latent, out_grad, offsets):
    rows, heads, width = queries.shape
    keys, full = latent.shape
    nope = w_uk.shape[1]
    lat = w_uk.shape[2]
    values = out_grad.shape[2]
    scale = 1.0 / math.sqrt(width)
    wide = heads * rows
    group = 4 if heads % 4 == 0 else heads
    groups = heads // group
    span = group * rows
    tile = min(TILE, keys)
    tiles = keys // tile
    block = min(BLOCK, keys)
    blocks = keys // block
    off = (offsets - lax.axis_index("key") * keys).reshape(1, rows)
    flipped = latent.T
    e, dp, qc, dl, st, tops = pl.pallas_call(
        functools.partial(scores_kernel, scale, group, tile),
        grid=(groups,),
        in_specs=[
            vmem((group, width, rows), lambda i: (i, 0, 0)),
            vmem((group, rows, values), lambda i: (i, 0, 0)),
            vmem((group, nope, lat), lambda i: (i, 0, 0)),
            vmem((group, lat, values), lambda i: (i, 0, 0)),
            vmem((full, keys), lambda i: (0, 0)),
            vmem((1, rows), lambda i: (0, 0)),
        ],
        out_specs=[
            vmem((keys, span), lambda i: (0, i)),
            vmem((keys, span), lambda i: (0, i)),
            vmem((full, span), lambda i: (0, i)),
            vmem((lat, span), lambda i: (0, i)),
            vmem((3, heads, rows), lambda i: (0, 0, 0)),
            vmem((tiles, heads, rows), lambda i: (0, 0, 0)),
        ],
        out_shape=[
            jax.ShapeDtypeStruct((keys, wide), bf16),
            jax.ShapeDtypeStruct((keys, wide), bf16),
            jax.ShapeDtypeStruct((full, wide), bf16),
            jax.ShapeDtypeStruct((lat, wide), bf16),
            jax.ShapeDtypeStruct((3, heads, rows), f32),
            jax.ShapeDtypeStruct((tiles, heads, rows), f32),
        ],
        scratch_shapes=[pltpu.VMEM((keys, full), bf16)],
        compiler_params=pltpu.CompilerParams(vmem_limit_bytes=VMEM_BYTES),
    )(queries.transpose(1, 2, 0), out_grad.transpose(1, 0, 2), w_uk, w_uv, flipped, off)
    bits = head_n.bit_length() - 1
    chunk = rows // key_n
    piece = full // head_n
    dma = pltpu.SemaphoreType.DMA
    anywhere = pl.BlockSpec(memory_space=pl.ANY)
    d_latent, dq = pl.pallas_call(
        functools.partial(grads_kernel, scale, key_n, head_n, rows, tile, block, group),
        in_specs=[anywhere] * 6 + [vmem(), vmem()],
        out_specs=[vmem(), vmem()],
        out_shape=[
            jax.ShapeDtypeStruct((blocks, head_n, piece, block), bf16),
            jax.ShapeDtypeStruct((groups, group, chunk, width), bf16),
        ],
        scratch_shapes=[
            pltpu.VMEM((keys, wide), bf16),
            pltpu.VMEM((keys, wide), bf16),
            pltpu.VMEM((full, wide), bf16),
            pltpu.VMEM((lat, wide), bf16),
            pltpu.VMEM((full, keys), bf16),
            pltpu.VMEM((heads, nope, lat), bf16),
            pltpu.VMEM((tiles, heads, rows), f32),
            pltpu.VMEM((heads, rows), f32),
            pltpu.VMEM((blocks, head_n, piece, block), bf16),
            pltpu.VMEM((blocks, head_n, piece, block), bf16),
            pltpu.VMEM((key_n, groups, group, chunk, width), bf16),
            pltpu.VMEM((key_n - 1, groups, group, chunk, width), bf16),
            pltpu.VMEM((key_n - 1, 3, heads, rows), f32),
            dma((blocks,)),
            dma((blocks,)),
            dma((4,)),
            dma((key_n - 1,)),
            dma((key_n - 1,)),
            dma((blocks, bits)),
            dma((blocks, bits)),
            dma((blocks, bits)),
            dma((blocks, bits)),
            dma((key_n - 1, groups)),
            dma((key_n - 1, groups)),
        ],
        compiler_params=pltpu.CompilerParams(
            vmem_limit_bytes=VMEM_BYTES, collective_id=0, has_side_effects=True
        ),
    )(e, dp, qc, dl, flipped, w_uk, st, tops)
    d_latent = d_latent.transpose(1, 2, 0, 3).reshape(full, keys).T
    return (dq.reshape(heads, chunk, width).transpose(1, 0, 2), d_latent)


def solution(mesh):
    return jax.shard_map(
        functools.partial(shards, mesh.shape["key"], mesh.shape["head"]),
        mesh=mesh,
        in_specs=(
            P(None, "head", None),
            P("head", None, None),
            P("head", None, None),
            P("key", None),
            P(None, "head", None),
            P(),
        ),
        out_specs=(P("key", "head", None), P("key", None)),
        check_vma=False,
    )
```

```python
import functools
import math

import jax
import jax.numpy as jnp
from jax import lax
from jax.experimental import pallas as pl
from jax.experimental.pallas import tpu as pltpu
from jax.sharding import PartitionSpec as P

floor_score = -1e30
MESH = pl.DeviceIdType.MESH
f32 = jnp.float32
bf16 = jnp.bfloat16
VMEM_BYTES = 60 * 1024 * 1024
TILE = 512
BLOCK = 512


def dot(a, b):
    return lax.dot_general(a, b, (((1,), (0,)), ((), ())), preferred_element_type=f32)


def dot_t(a, b):
    return lax.dot_general(a, b, (((1,), (1,)), ((), ())), preferred_element_type=f32)
LONG = (2, 5)


def dot_c(a, b):
    return lax.dot_general(a, b, (((0,), (0,)), ((), ())), preferred_element_type=f32)


def scores_kernel(
    scale, group, tile, q_ref, og_ref, uk_ref, uv_ref, lt_ref, off_ref,
    e_ref, dp_ref, qc_ref, dl_ref, st_ref, tops_ref, lat_ref,
):
    step = pl.program_id(0)
    rows = q_ref.shape[2]
    nope = uk_ref.shape[1]
    width = uk_ref.shape[2]
    keys = lt_ref.shape[1]

    @pl.when(step == 0)
    def _():
        lat_ref[...] = lt_ref[...].T

    for h in range(group):
        cut = slice(h * rows, (h + 1) * rows)
        qc_ref[:width, cut] = dot_c(uk_ref[h], q_ref[h, :nope, :]).astype(bf16)
        qc_ref[width:, cut] = q_ref[h, nope:, :]
        dl_ref[:, cut] = dot_t(uv_ref[h], og_ref[h]).astype(bf16)
    qc = qc_ref[...]
    dl = dl_ref[...]
    unit = scale * math.log2(math.e)
    off = jnp.concatenate([off_ref[...] - lax.axis_index("key") * keys] * group, axis=1)
    tops = []
    totals = []
    accs = []
    for t in range(keys // tile):
        at = pl.ds(t * tile, tile)
        s = dot(lat_ref[at, :], qc)
        dp = dot(lat_ref[at, :width], dl).astype(bf16)
        position = lax.broadcasted_iota(jnp.int32, s.shape, 0)
        s = jnp.where(position <= off - t * tile, s, floor_score)
        top = jnp.maximum(jnp.max(s, axis=0, keepdims=True), 0.5 * floor_score)
        e = jnp.exp2((s - top) * unit).astype(bf16)
        e_ref[at, :] = e
        dp_ref[at, :] = dp
        e = e.astype(f32)
        tops.append(top * unit)
        totals.append(jnp.sum(e, axis=0, keepdims=True))
        accs.append(jnp.sum(e * dp.astype(f32), axis=0, keepdims=True))
    best = functools.reduce(jnp.maximum, tops)
    total = 0.0
    acc = 0.0
    for top, a, b in zip(tops, totals, accs):
        near = jnp.exp2(top - best)
        total = total + near * a
        acc = acc + near * b
    for h in range(group):
        cut = slice(h * rows, (h + 1) * rows)
        at = pl.ds(step * group + h, 1)
        st_ref[0, at, :] = best[:, cut]
        st_ref[1, at, :] = total[:, cut]
        st_ref[2, at, :] = acc[:, cut]
        for t, top in enumerate(tops):
            tops_ref[t, at, :] = top[:, cut]


def grads_kernel(
    scale, key_n, head_n, rows, tile, block, group,
    e_hbm, dp_hbm, qc_hbm, dl_hbm, lt_hbm, uk_hbm, st_ref, tops_ref,
    out_ref, dqo_ref,
    e_ref, dp_ref, qc_ref, dl_ref, lt_ref, uk_ref, norm_ref, delta_ref, part_ref, got_ref,
    dq_ref, dqg_ref, stg_ref,
    e_sem, dp_sem, in_sem, st_send, st_recv, rs_send, rs_recv, ag_send, ag_recv, q_send, q_recv,
):
    mk = lax.axis_index("key")
    mh = lax.axis_index("head")
    bits = head_n.bit_length() - 1
    keys = e_ref.shape[0]
    wide = e_ref.shape[1]
    width = dl_ref.shape[0]
    nope = uk_ref.shape[1]
    full = qc_ref.shape[0]
    blocks = keys // block
    span = group * rows
    groups = wide // span
    piece = full // head_n
    chunk = rows // key_n
    rotary = full - width
    pair = nope // rotary

    def bit(b):
        return lax.rem(lax.div(mh, 1 << b), 2)

    def partner(b):
        return mh + (1 - 2 * bit(b)) * (1 << b)

    barrier = pltpu.get_barrier_semaphore()
    for d in range(1, key_n):
        pl.semaphore_signal(
            barrier, inc=1, device_id={"key": lax.rem(mk + d, key_n)}, device_id_type=MESH
        )
    for b in range(bits):
        pl.semaphore_signal(
            barrier, inc=1, device_id={"head": partner(b)}, device_id_type=MESH
        )

    def local(a, b, sem):
        copy = pltpu.make_async_copy(a, b, sem)
        copy.start()
        return copy

    e_in = []
    dp_in = []
    weights = []
    for b in range(blocks):
        at = pl.ds(b * block, block)
        e_in.append(local(e_hbm.at[at], e_ref.at[at], e_sem.at[b]))
        dp_in.append(local(dp_hbm.at[at], dp_ref.at[at], dp_sem.at[b]))
        if b == 0:
            weights.append(local(qc_hbm, qc_ref, in_sem.at[0]))
            weights.append(local(dl_hbm, dl_ref, in_sem.at[1]))
    weights.append(local(lt_hbm, lt_ref, in_sem.at[2]))
    weights.append(local(uk_hbm, uk_ref, in_sem.at[3]))

    pl.semaphore_wait(barrier, key_n - 1 + bits)

    def remote(src, dst, send, recv, where):
        copy = pltpu.make_async_remote_copy(
            src_ref=src, dst_ref=dst, send_sem=send, recv_sem=recv,
            device_id=where, device_id_type=MESH,
        )
        copy.start()
        return copy

    copies = []
    for d in range(1, key_n):
        copies.append(
            remote(
                st_ref, stg_ref.at[d - 1], st_send.at[d - 1], st_recv.at[d - 1],
                {"key": lax.rem(mk + d, key_n)},
            )
        )
    for copy in copies:
        copy.wait()
    best = st_ref[0]
    for d in range(key_n - 1):
        best = jnp.maximum(best, stg_ref[d, 0])
    near = jnp.exp2(st_ref[0] - best)
    total = near * st_ref[1]
    acc = near * st_ref[2]
    for d in range(key_n - 1):
        near = jnp.exp2(stg_ref[d, 0] - best)
        total = total + near * stg_ref[d, 1]
        acc = acc + near * stg_ref[d, 2]
    delta_ref[...] = acc / total
    for t in range(keys // tile):
        norm_ref[t] = jnp.exp2(tops_ref[t] - best) / total

    def row(ref, g, t=None):
        pick = (lambda i: ref[pl.ds(i, 1), :]) if t is None else (lambda i: ref[t, pl.ds(i, 1), :])
        return jnp.concatenate([pick(g * group + h) for h in range(group)], axis=1)

    def prepare(b):
        e_in[b].wait()
        dp_in[b].wait()
        at = pl.ds(b * block, block)
        for g in range(groups):
            cut = slice(g * span, (g + 1) * span)
            p = e_ref[at, cut].astype(f32) * row(norm_ref, g, b * block // tile)
            e_ref[at, cut] = p.astype(bf16)
            dp_ref[at, cut] = (p * (dp_ref[at, cut].astype(f32) - row(delta_ref, g))).astype(bf16)

    def latent_block(b):
        if b == 0:
            weights[0].wait()
            weights[1].wait()
        if b + 1 < blocks:
            prepare(b + 1)
        at = pl.ds(b * block, block)
        from_scores = dot_t(qc_ref[...], dp_ref[at, :]) * scale
        from_values = dot_t(dl_ref[...], e_ref[at, :])
        summed = jnp.concatenate(
            [from_scores[:width] + from_values, from_scores[width:]], axis=0
        )
        for j in range(head_n):
            part_ref[b, j] = summed[j * piece : (j + 1) * piece].astype(bf16)

    q_copies = []

    def query_group(g):
        if g == 0:
            weights[2].wait()
            weights[3].wait()
        cut = slice(g * span, (g + 1) * span)
        dq = dot(lt_ref[...], dp_ref[:, cut]) * scale
        high = dq[:width].astype(bf16)
        low = (dq[:width] - high.astype(f32)).astype(bf16)
        for h in range(group):
            mine = slice(h * rows, (h + 1) * rows)
            w = uk_ref[g * group + h]
            a = (dot(w, high[:, mine]) + dot(w, low[:, mine])).T
            for j in range(key_n):
                dq_ref[j, g, h] = a[j * chunk : (j + 1) * chunk].astype(bf16)
        for i in range(group // pair):
            mine = [slice(h * rows, (h + 1) * rows) for h in range(i * pair, (i + 1) * pair)]
            a = jnp.concatenate([dq[width:, m] for m in mine], axis=0).T
            for j in range(key_n):
                dq_ref[j, g, group + i] = a[j * chunk : (j + 1) * chunk].astype(bf16)
        for d in range(1, key_n):
            to = lax.rem(mk + d, key_n)
            q_copies.append(
                remote(
                    dq_ref.at[to, g], dqg_ref.at[d - 1, g],
                    q_send.at[d - 1, g], q_recv.at[d - 1, g], {"key": to},
                )
            )

    orders = [[0] + list(range(1, bits)), [0] + list(range(bits - 1, 0, -1))]
    flight = [None] * blocks
    base = [0] * blocks
    stage = [0] * blocks

    def advance(b):
        k = stage[b]
        order = orders[b % 2]
        if k > 0:
            flight[b].wait()
        if 0 < k <= bits:
            size = head_n >> k
            spot = head_n - (head_n >> (k - 1))
            for j in range(size):
                summed = part_ref[b, base[b] + j].astype(f32) + got_ref[b, spot + j].astype(f32)
                if k == bits:
                    out_ref[base[b] + j, :, b * block : (b + 1) * block] = summed.astype(bf16)
                else:
                    part_ref[b, base[b] + j] = summed.astype(bf16)
        if k < bits:
            size = head_n >> (k + 1)
            spot = head_n - (head_n >> k)
            v = bit(order[k])
            flight[b] = remote(
                part_ref.at[b, pl.ds(base[b] + (1 - v) * size, size)],
                got_ref.at[b, pl.ds(spot, size)],
                rs_send.at[b, k], rs_recv.at[b, k], {"head": partner(order[k])},
            )
            base[b] = base[b] + v * size
        elif k < 2 * bits:
            i = k - bits
            size = 1 << i
            if i > 0:
                base[b] = base[b] - bit(order[bits - i]) * (size // 2)
            at = out_ref.at[pl.ds(base[b], size), :, pl.ds(b * block, block)]
            flight[b] = remote(
                at, at,
                ag_send.at[b, i], ag_recv.at[b, i], {"head": partner(order[bits - 1 - i])},
            )
        stage[b] = k + 1

    age = [0] * blocks
    ready = [False] * blocks

    def sweep(drain):
        for b in range(blocks):
            if ready[b] and stage[b] <= 2 * bits:
                age[b] += 1
                if drain or age[b] > (stage[b] in LONG):
                    advance(b)
                    age[b] = 0

    work = [(latent_block, b) for b in range(blocks)]
    work = work[:-1] + [(query_group, 0)] + work[-1:]
    work += [(query_group, g) for g in range(1, groups)]
    prepare(0)
    for do, i in work:
        do(i)
        if do is latent_block:
            ready[i] = True
        sweep(False)
    while min(stage) <= 2 * bits:
        sweep(True)
    for copy in q_copies:
        copy.wait()
    for g in range(groups):
        summed = dq_ref[mk, g].astype(f32)
        for d in range(key_n - 1):
            summed = summed + dqg_ref[d, g].astype(f32)
        summed = summed.astype(bf16)
        for h in range(group):
            dqo_ref[g, h, :, :nope] = summed[h]
            cut = slice(h % pair * rotary, (h % pair + 1) * rotary)
            dqo_ref[g, h, :, nope:] = summed[group + h // pair][:, cut]


def vmem(shape=None, index=None):
    return pl.BlockSpec(shape, index, memory_space=pltpu.VMEM)


def shards(key_n, head_n, queries, w_uk, w_uv, latent, out_grad, offsets):
    rows, heads, width = queries.shape
    keys, full = latent.shape
    nope = w_uk.shape[1]
    lat = w_uk.shape[2]
    values = out_grad.shape[2]
    scale = 1.0 / math.sqrt(width)
    wide = heads * rows
    group = 4 if heads % 4 == 0 else heads
    groups = heads // group
    span = group * rows
    tile = min(TILE, keys)
    tiles = keys // tile
    block = min(BLOCK, keys)
    blocks = keys // block
    off = offsets.reshape(1, rows)
    flipped = latent.T
    e, dp, qc, dl, st, tops = pl.pallas_call(
        functools.partial(scores_kernel, scale, group, tile),
        grid=(groups,),
        in_specs=[
            vmem((group, width, rows), lambda i: (i, 0, 0)),
            vmem((group, rows, values), lambda i: (i, 0, 0)),
            vmem((group, nope, lat), lambda i: (i, 0, 0)),
            vmem((group, lat, values), lambda i: (i, 0, 0)),
            vmem((full, keys), lambda i: (0, 0)),
            vmem((1, rows), lambda i: (0, 0)),
        ],
        out_specs=[
            vmem((keys, span), lambda i: (0, i)),
            vmem((keys, span), lambda i: (0, i)),
            vmem((full, span), lambda i: (0, i)),
            vmem((lat, span), lambda i: (0, i)),
            vmem((3, heads, rows), lambda i: (0, 0, 0)),
            vmem((tiles, heads, rows), lambda i: (0, 0, 0)),
        ],
        out_shape=[
            jax.ShapeDtypeStruct((keys, wide), bf16),
            jax.ShapeDtypeStruct((keys, wide), bf16),
            jax.ShapeDtypeStruct((full, wide), bf16),
            jax.ShapeDtypeStruct((lat, wide), bf16),
            jax.ShapeDtypeStruct((3, heads, rows), f32),
            jax.ShapeDtypeStruct((tiles, heads, rows), f32),
        ],
        scratch_shapes=[pltpu.VMEM((keys, full), bf16)],
        compiler_params=pltpu.CompilerParams(vmem_limit_bytes=VMEM_BYTES),
    )(queries.transpose(1, 2, 0), out_grad.transpose(1, 0, 2), w_uk, w_uv, flipped, off)
    bits = head_n.bit_length() - 1
    chunk = rows // key_n
    piece = full // head_n
    slots = group + group * (full - lat) // nope
    dma = pltpu.SemaphoreType.DMA
    anywhere = pl.BlockSpec(memory_space=pl.ANY)
    d_latent, dq = pl.pallas_call(
        functools.partial(grads_kernel, scale, key_n, head_n, rows, tile, block, group),
        in_specs=[anywhere] * 6 + [vmem(), vmem()],
        out_specs=[vmem(), vmem()],
        out_shape=[
            jax.ShapeDtypeStruct((head_n, piece, keys), bf16),
            jax.ShapeDtypeStruct((groups, group, chunk, width), bf16),
        ],
        scratch_shapes=[
            pltpu.VMEM((keys, wide), bf16),
            pltpu.VMEM((keys, wide), bf16),
            pltpu.VMEM((full, wide), bf16),
            pltpu.VMEM((lat, wide), bf16),
            pltpu.VMEM((full, keys), bf16),
            pltpu.VMEM((heads, nope, lat), bf16),
            pltpu.VMEM((tiles, heads, rows), f32),
            pltpu.VMEM((heads, rows), f32),
            pltpu.VMEM((blocks, head_n, piece, block), bf16),
            pltpu.VMEM((blocks, head_n, piece, block), bf16),
            pltpu.VMEM((key_n, groups, slots, chunk, nope), bf16),
            pltpu.VMEM((key_n - 1, groups, slots, chunk, nope), bf16),
            pltpu.VMEM((key_n - 1, 3, heads, rows), f32),
            dma((blocks,)),
            dma((blocks,)),
            dma((4,)),
            dma((key_n - 1,)),
            dma((key_n - 1,)),
            dma((blocks, bits)),
            dma((blocks, bits)),
            dma((blocks, bits)),
            dma((blocks, bits)),
            dma((key_n - 1, groups)),
            dma((key_n - 1, groups)),
        ],
        compiler_params=pltpu.CompilerParams(
            vmem_limit_bytes=VMEM_BYTES, collective_id=0, has_side_effects=True
        ),
    )(e, dp, qc, dl, flipped, w_uk, st, tops)
    d_latent = d_latent.reshape(full, keys).T
    return (dq.reshape(heads, chunk, width).transpose(1, 0, 2), d_latent)


def solution(mesh):
    return jax.shard_map(
        functools.partial(shards, mesh.shape["key"], mesh.shape["head"]),
        mesh=mesh,
        in_specs=(
            P(None, "head", None),
            P("head", None, None),
            P("head", None, None),
            P("key", None),
            P(None, "head", None),
            P(),
        ),
        out_specs=(P("key", "head", None), P("key", None)),
        check_vma=False,
    )
```

```python
import functools
import math

import jax
import jax.numpy as jnp
from jax import lax
from jax.experimental import pallas as pl
from jax.experimental.pallas import tpu as pltpu
from jax.sharding import PartitionSpec as P

floor_score = -1e30
MESH = pl.DeviceIdType.MESH
f32 = jnp.float32
bf16 = jnp.bfloat16
VMEM_BYTES = 60 * 1024 * 1024
TILE = 512
BLOCK = 512


def dot(a, b):
    return lax.dot_general(a, b, (((1,), (0,)), ((), ())), preferred_element_type=f32)


def dot_t(a, b):
    return lax.dot_general(a, b, (((1,), (1,)), ((), ())), preferred_element_type=f32)
LONG = ()


def dot_c(a, b):
    return lax.dot_general(a, b, (((0,), (0,)), ((), ())), preferred_element_type=f32)


def scores_kernel(
    scale, group, tile, q_ref, og_ref, uk_ref, uv_ref, lt_ref, off_ref,
    e_ref, dp_ref, qc_ref, dl_ref, st_ref, tops_ref, lat_ref,
):
    step = pl.program_id(0)
    rows = q_ref.shape[2]
    nope = uk_ref.shape[1]
    width = uk_ref.shape[2]
    keys = lt_ref.shape[1]

    @pl.when(step == 0)
    def _():
        lat_ref[...] = lt_ref[...].T

    for h in range(group):
        cut = slice(h * rows, (h + 1) * rows)
        qc_ref[:width, cut] = dot_c(uk_ref[h], q_ref[h, :nope, :]).astype(bf16)
        qc_ref[width:, cut] = q_ref[h, nope:, :]
        dl_ref[:, cut] = dot_t(uv_ref[h], og_ref[h]).astype(bf16)
    qc = qc_ref[...]
    dl = dl_ref[...]
    unit = scale * math.log2(math.e)
    off = jnp.concatenate([off_ref[...] - lax.axis_index("key") * keys] * group, axis=1)
    tops = []
    totals = []
    accs = []
    for t in range(keys // tile):
        at = pl.ds(t * tile, tile)
        s = dot(lat_ref[at, :], qc)
        dp = dot(lat_ref[at, :width], dl).astype(bf16)
        position = lax.broadcasted_iota(jnp.int32, s.shape, 0)
        s = jnp.where(position <= off - t * tile, s, floor_score)
        top = jnp.maximum(jnp.max(s, axis=0, keepdims=True), 0.5 * floor_score)
        e = jnp.exp2((s - top) * unit).astype(bf16)
        e_ref[at, :] = e
        dp_ref[at, :] = dp
        e = e.astype(f32)
        tops.append(top * unit)
        totals.append(jnp.sum(e, axis=0, keepdims=True))
        accs.append(jnp.sum(e * dp.astype(f32), axis=0, keepdims=True))
    best = functools.reduce(jnp.maximum, tops)
    total = 0.0
    acc = 0.0
    for top, a, b in zip(tops, totals, accs):
        near = jnp.exp2(top - best)
        total = total + near * a
        acc = acc + near * b
    for h in range(group):
        cut = slice(h * rows, (h + 1) * rows)
        at = pl.ds(step * group + h, 1)
        st_ref[0, at, :] = best[:, cut]
        st_ref[1, at, :] = total[:, cut]
        st_ref[2, at, :] = acc[:, cut]
        for t, top in enumerate(tops):
            tops_ref[t, at, :] = top[:, cut]


def grads_kernel(
    scale, key_n, head_n, rows, tile, block, group,
    e_hbm, dp_hbm, qc_hbm, dl_hbm, lt_hbm, uk_hbm, st_ref, tops_ref,
    out_ref, dqo_ref,
    e_ref, dp_ref, qc_ref, dl_ref, lt_ref, uk_ref, norm_ref, delta_ref, part_ref, got_ref, gat_ref,
    dq_ref, dqg_ref, stg_ref,
    e_sem, dp_sem, in_sem, st_send, st_recv, rs_send, rs_recv, ag_send, ag_recv, q_send, q_recv,
):
    mk = lax.axis_index("key")
    mh = lax.axis_index("head")
    bits = head_n.bit_length() - 1
    keys = e_ref.shape[0]
    wide = e_ref.shape[1]
    width = dl_ref.shape[0]
    nope = uk_ref.shape[1]
    full = qc_ref.shape[0]
    blocks = keys // block
    span = group * rows
    groups = wide // span
    piece = full // head_n
    chunk = rows // key_n
    rotary = full - width
    pair = nope // rotary

    def bit(b):
        return lax.rem(lax.div(mh, 1 << b), 2)

    def partner(b):
        return mh + (1 - 2 * bit(b)) * (1 << b)

    barrier = pltpu.get_barrier_semaphore()
    for d in range(1, key_n):
        pl.semaphore_signal(
            barrier, inc=1, device_id={"key": lax.rem(mk + d, key_n)}, device_id_type=MESH
        )
    for b in range(bits):
        pl.semaphore_signal(
            barrier, inc=1, device_id={"head": partner(b)}, device_id_type=MESH
        )

    def local(a, b, sem):
        copy = pltpu.make_async_copy(a, b, sem)
        copy.start()
        return copy

    e_in = []
    dp_in = []
    weights = []
    for b in range(blocks):
        at = pl.ds(b * block, block)
        e_in.append(local(e_hbm.at[at], e_ref.at[at], e_sem.at[b]))
        dp_in.append(local(dp_hbm.at[at], dp_ref.at[at], dp_sem.at[b]))
        if b == 0:
            weights.append(local(qc_hbm, qc_ref, in_sem.at[0]))
            weights.append(local(dl_hbm, dl_ref, in_sem.at[1]))
    weights.append(local(lt_hbm, lt_ref, in_sem.at[2]))
    weights.append(local(uk_hbm, uk_ref, in_sem.at[3]))

    pl.semaphore_wait(barrier, key_n - 1 + bits)

    def remote(src, dst, send, recv, where):
        copy = pltpu.make_async_remote_copy(
            src_ref=src, dst_ref=dst, send_sem=send, recv_sem=recv,
            device_id=where, device_id_type=MESH,
        )
        copy.start()
        return copy

    copies = []
    for d in range(1, key_n):
        copies.append(
            remote(
                st_ref, stg_ref.at[d - 1], st_send.at[d - 1], st_recv.at[d - 1],
                {"key": lax.rem(mk + d, key_n)},
            )
        )
    for copy in copies:
        copy.wait()
    best = st_ref[0]
    for d in range(key_n - 1):
        best = jnp.maximum(best, stg_ref[d, 0])
    near = jnp.exp2(st_ref[0] - best)
    total = near * st_ref[1]
    acc = near * st_ref[2]
    for d in range(key_n - 1):
        near = jnp.exp2(stg_ref[d, 0] - best)
        total = total + near * stg_ref[d, 1]
        acc = acc + near * stg_ref[d, 2]
    delta_ref[...] = acc / total
    for t in range(keys // tile):
        norm_ref[t] = jnp.exp2(tops_ref[t] - best) / total

    def row(ref, g, t=None):
        pick = (lambda i: ref[pl.ds(i, 1), :]) if t is None else (lambda i: ref[t, pl.ds(i, 1), :])
        return jnp.concatenate([pick(g * group + h) for h in range(group)], axis=1)

    def prepare(b):
        e_in[b].wait()
        dp_in[b].wait()
        at = pl.ds(b * block, block)
        for g in range(groups):
            cut = slice(g * span, (g + 1) * span)
            p = e_ref[at, cut].astype(f32) * row(norm_ref, g, b * block // tile)
            e_ref[at, cut] = p.astype(bf16)
            dp_ref[at, cut] = (p * (dp_ref[at, cut].astype(f32) - row(delta_ref, g))).astype(bf16)

    def latent_block(b):
        if b == 0:
            weights[0].wait()
            weights[1].wait()
        prepare(b)
        at = pl.ds(b * block, block)
        from_scores = dot_t(qc_ref[...], dp_ref[at, :]) * scale
        from_values = dot_t(dl_ref[...], e_ref[at, :])
        summed = jnp.concatenate(
            [from_scores[:width] + from_values, from_scores[width:]], axis=0
        )
        for j in range(head_n):
            part_ref[b, j] = summed[j * piece : (j + 1) * piece].astype(bf16)

    q_copies = []

    def query_group(g):
        if g == 0:
            weights[2].wait()
            weights[3].wait()
        cut = slice(g * span, (g + 1) * span)
        dq = dot(lt_ref[...], dp_ref[:, cut]) * scale
        high = dq[:width].astype(bf16)
        low = (dq[:width] - high.astype(f32)).astype(bf16)
        for h in range(group):
            mine = slice(h * rows, (h + 1) * rows)
            w = uk_ref[g * group + h]
            a = (dot(w, high[:, mine]) + dot(w, low[:, mine])).T
            for j in range(key_n):
                dq_ref[j, g, h] = a[j * chunk : (j + 1) * chunk].astype(bf16)
        for i in range(group // pair):
            mine = [slice(h * rows, (h + 1) * rows) for h in range(i * pair, (i + 1) * pair)]
            a = jnp.concatenate([dq[width:, m] for m in mine], axis=0).T
            for j in range(key_n):
                dq_ref[j, g, group + i] = a[j * chunk : (j + 1) * chunk].astype(bf16)
        for d in range(1, key_n):
            to = lax.rem(mk + d, key_n)
            q_copies.append(
                remote(
                    dq_ref.at[to, g], dqg_ref.at[d - 1, g],
                    q_send.at[d - 1, g], q_recv.at[d - 1, g], {"key": to},
                )
            )

    orders = [[0] + list(range(1, bits)), [0] + list(range(bits - 1, 0, -1))]
    flight = [None] * blocks
    base = [0] * blocks
    stage = [0] * blocks

    def advance(b):
        k = stage[b]
        order = orders[b % 2]
        if k > 0:
            flight[b].wait()
        if 0 < k <= bits:
            size = head_n >> k
            spot = head_n - (head_n >> (k - 1))
            for j in range(size):
                summed = part_ref[b, base[b] + j].astype(f32) + got_ref[b, spot + j].astype(f32)
                if k == bits:
                    gat_ref[b, base[b] + j] = summed.astype(bf16)
                else:
                    part_ref[b, base[b] + j] = summed.astype(bf16)
        if k < bits:
            size = head_n >> (k + 1)
            spot = head_n - (head_n >> k)
            v = bit(order[k])
            flight[b] = remote(
                part_ref.at[b, pl.ds(base[b] + (1 - v) * size, size)],
                got_ref.at[b, pl.ds(spot, size)],
                rs_send.at[b, k], rs_recv.at[b, k], {"head": partner(order[k])},
            )
            base[b] = base[b] + v * size
        elif k < 2 * bits:
            i = k - bits
            size = 1 << i
            if i > 0:
                base[b] = base[b] - bit(order[bits - i]) * (size // 2)
            at = gat_ref.at[b, pl.ds(base[b], size)]
            flight[b] = remote(
                at, at,
                ag_send.at[b, i], ag_recv.at[b, i], {"head": partner(order[bits - 1 - i])},
            )
        elif k == 2 * bits:
            for j in range(head_n):
                out_ref[j, :, b * block : (b + 1) * block] = gat_ref[b, j]
        stage[b] = k + 1

    age = [0] * blocks
    ready = [False] * blocks

    def sweep(drain):
        for b in range(blocks):
            if ready[b] and stage[b] <= 2 * bits:
                age[b] += 1
                if drain or age[b] > (stage[b] in LONG):
                    advance(b)
                    age[b] = 0

    work = [(latent_block, b) for b in range(blocks)]
    work += [(query_group, g) for g in range(groups)]
    for do, i in work:
        do(i)
        if do is latent_block:
            ready[i] = True
        sweep(False)
    while min(stage) <= 2 * bits:
        sweep(True)
    for copy in q_copies:
        copy.wait()
    for g in range(groups):
        summed = dq_ref[mk, g].astype(f32)
        for d in range(key_n - 1):
            summed = summed + dqg_ref[d, g].astype(f32)
        summed = summed.astype(bf16)
        for h in range(group):
            dqo_ref[g, h, :, :nope] = summed[h]
            cut = slice(h % pair * rotary, (h % pair + 1) * rotary)
            dqo_ref[g, h, :, nope:] = summed[group + h // pair][:, cut]


def vmem(shape=None, index=None):
    return pl.BlockSpec(shape, index, memory_space=pltpu.VMEM)


def shards(key_n, head_n, queries, w_uk, w_uv, latent, out_grad, offsets):
    rows, heads, width = queries.shape
    keys, full = latent.shape
    nope = w_uk.shape[1]
    lat = w_uk.shape[2]
    values = out_grad.shape[2]
    scale = 1.0 / math.sqrt(width)
    wide = heads * rows
    group = 4 if heads % 4 == 0 else heads
    groups = heads // group
    span = group * rows
    tile = min(TILE, keys)
    tiles = keys // tile
    block = min(BLOCK, keys)
    blocks = keys // block
    off = offsets.reshape(1, rows)
    flipped = latent.T
    e, dp, qc, dl, st, tops = pl.pallas_call(
        functools.partial(scores_kernel, scale, group, tile),
        grid=(groups,),
        in_specs=[
            vmem((group, width, rows), lambda i: (i, 0, 0)),
            vmem((group, rows, values), lambda i: (i, 0, 0)),
            vmem((group, nope, lat), lambda i: (i, 0, 0)),
            vmem((group, lat, values), lambda i: (i, 0, 0)),
            vmem((full, keys), lambda i: (0, 0)),
            vmem((1, rows), lambda i: (0, 0)),
        ],
        out_specs=[
            vmem((keys, span), lambda i: (0, i)),
            vmem((keys, span), lambda i: (0, i)),
            vmem((full, span), lambda i: (0, i)),
            vmem((lat, span), lambda i: (0, i)),
            vmem((3, heads, rows), lambda i: (0, 0, 0)),
            vmem((tiles, heads, rows), lambda i: (0, 0, 0)),
        ],
        out_shape=[
            jax.ShapeDtypeStruct((keys, wide), bf16),
            jax.ShapeDtypeStruct((keys, wide), bf16),
            jax.ShapeDtypeStruct((full, wide), bf16),
            jax.ShapeDtypeStruct((lat, wide), bf16),
            jax.ShapeDtypeStruct((3, heads, rows), f32),
            jax.ShapeDtypeStruct((tiles, heads, rows), f32),
        ],
        scratch_shapes=[pltpu.VMEM((keys, full), bf16)],
        compiler_params=pltpu.CompilerParams(vmem_limit_bytes=VMEM_BYTES),
    )(queries.transpose(1, 2, 0), out_grad.transpose(1, 0, 2), w_uk, w_uv, flipped, off)
    bits = head_n.bit_length() - 1
    chunk = rows // key_n
    piece = full // head_n
    slots = group + group * (full - lat) // nope
    dma = pltpu.SemaphoreType.DMA
    anywhere = pl.BlockSpec(memory_space=pl.ANY)
    d_latent, dq = pl.pallas_call(
        functools.partial(grads_kernel, scale, key_n, head_n, rows, tile, block, group),
        in_specs=[anywhere] * 6 + [vmem(), vmem()],
        out_specs=[vmem(), vmem()],
        out_shape=[
            jax.ShapeDtypeStruct((head_n, piece, keys), bf16),
            jax.ShapeDtypeStruct((groups, group, chunk, width), bf16),
        ],
        scratch_shapes=[
            pltpu.VMEM((keys, wide), bf16),
            pltpu.VMEM((keys, wide), bf16),
            pltpu.VMEM((full, wide), bf16),
            pltpu.VMEM((lat, wide), bf16),
            pltpu.VMEM((full, keys), bf16),
            pltpu.VMEM((heads, nope, lat), bf16),
            pltpu.VMEM((tiles, heads, rows), f32),
            pltpu.VMEM((heads, rows), f32),
            pltpu.VMEM((blocks, head_n, piece, block), bf16),
            pltpu.VMEM((blocks, head_n, piece, block), bf16),
            pltpu.VMEM((blocks, head_n, piece, block), bf16),
            pltpu.VMEM((key_n, groups, slots, chunk, nope), bf16),
            pltpu.VMEM((key_n - 1, groups, slots, chunk, nope), bf16),
            pltpu.VMEM((key_n - 1, 3, heads, rows), f32),
            dma((blocks,)),
            dma((blocks,)),
            dma((4,)),
            dma((key_n - 1,)),
            dma((key_n - 1,)),
            dma((blocks, bits)),
            dma((blocks, bits)),
            dma((blocks, bits)),
            dma((blocks, bits)),
            dma((key_n - 1, groups)),
            dma((key_n - 1, groups)),
        ],
        compiler_params=pltpu.CompilerParams(
            vmem_limit_bytes=VMEM_BYTES, collective_id=0, has_side_effects=True
        ),
    )(e, dp, qc, dl, flipped, w_uk, st, tops)
    d_latent = d_latent.reshape(full, keys).T
    return (dq.reshape(heads, chunk, width).transpose(1, 0, 2), d_latent)


def solution(mesh):
    return jax.shard_map(
        functools.partial(shards, mesh.shape["key"], mesh.shape["head"]),
        mesh=mesh,
        in_specs=(
            P(None, "head", None),
            P("head", None, None),
            P("head", None, None),
            P("key", None),
            P(None, "head", None),
            P(),
        ),
        out_specs=(P("key", "head", None), P("key", None)),
        check_vma=False,
    )
```
